32 devices in a mesh: group: 8 (over y, x, core), blk: 4 (over z).
Axes of the slice: x: 2, y: 2, z: 4, core: 2. Of those that a mesh axis runs over, the one named last changes fastest.
Arguments:
- front: float32 [8, 8192, 512], P('group', None, 'blk'), as said below
- child_blocks: float32 [8, 4, 8, 2, 128, 128], P('group', 'blk'), may hold values from -6 to 6
- child_rows: int32 [8, 4, 8, 2, 128], P('group', 'blk'), may hold values from 512 to 8191, as said below
- child_cols: int32 [8, 4, 8, 2, 128], P('group', 'blk'), may hold values from 0 to 127, each once within a row
- child_counts: int32 [8, 4, 8], P('group', 'blk'), may hold values from 0 to 2, as said below
Outputs:
- factors: float32 [8, 8192, 512], P('group', None, 'blk')
- pivots: float32 [8, 256], P('group')
The draws below stay inside these ranges and needn't reach their ends.
Inputs may be any that keep to these rules, and one draw needn't show every extreme that they name: Rows 0 to 511 of each front form a symmetric matrix whose leading 2 * 128 rows and columns have a positive diagonal that dominates every row of that block; rows from 512 on are unstructured. `child_rows`: the 128 row indices of one slot are distinct and lie at or below row 512. `child_counts`: for every column block some destination group receives 2 live slots from every source group.
All inputs are finite; a program needn't handle non-finite values.
Results may differ from the reference program's by a relative error of at most 0.0003.
Values sent between devices are 32-bit elements; how exact they have to be, the bound alone decides.
No kernel may reach another device: no remote copies, remote signals or barrier semaphores. Data moves between devices by JAX's collectives and lax.ppermute only.
A program may use at most 64 MiB of HBM per device.

```python
import jax
import jax.numpy as jnp
from jax import lax

BS = 128
F = 8192
PANELS = 2
CAP = 2
FRONTS = 8
BLOCKS = 4
WIN = 512


def draw_front(key, part):
    keys = jax.random.split(key, 5)
    panel_cols = PANELS * BS
    index_ids = jnp.arange(WIN)
    in_panel = index_ids < panel_cols
    both_panel = in_panel[:, None] & in_panel[None, :]
    both_rest = (~in_panel)[:, None] & (~in_panel)[None, :]
    scales = jnp.where(both_panel, 0.9 / panel_cols, jnp.where(both_rest, 0.1, 0.2))
    upper = jax.random.uniform(keys[1], (FRONTS, WIN, WIN), jnp.float32, -1.0, 1.0)
    sym = (upper + jnp.swapaxes(upper, 1, 2)) * 0.5
    panel_diag = jax.random.uniform(keys[0], (FRONTS, WIN), jnp.float32, 1.0, 2.0)
    rest_diag = jax.random.uniform(keys[4], (FRONTS, WIN), jnp.float32, 2.0, 4.0)
    diag_values = jnp.where(in_panel[None, :], panel_diag, rest_diag)
    identity = jnp.eye(WIN, dtype=jnp.float32)
    square = sym * scales[None] * (1.0 - identity)[None] + identity[None] * diag_values[:, :, None]
    below = jax.random.normal(keys[2], (FRONTS, F - WIN, WIN), jnp.float32)
    return jnp.concatenate([square, below], axis=1).astype(jnp.float32)


def draw_child_rows(key, part):
    count = FRONTS * BLOCKS * FRONTS * CAP
    keys = jax.random.split(key, count)
    picked = jax.vmap(lambda single: jax.random.permutation(single, F - WIN)[:BS])(keys)
    return (picked + WIN).reshape(FRONTS, BLOCKS, FRONTS, CAP, BS).astype(jnp.int32)


def draw_child_counts(key, part):
    keys = jax.random.split(key, 2)
    hottest = jax.random.randint(keys[0], (BLOCKS,), 0, FRONTS)
    base = jax.random.randint(keys[1], (FRONTS, BLOCKS, FRONTS), 0, CAP + 1)
    dest = jnp.arange(FRONTS)[None, None, :]
    return jnp.where(dest == hottest[None, :, None], CAP, base).astype(jnp.int32)


def block_scale(key, shape, cuts, least, largest):
    factor_of, own = 1.0, jax.random.fold_in(key, 6)
    for position, blocks in cuts:
        draws = jnp.exp(jax.random.uniform(jax.random.fold_in(own, position), (blocks,), jnp.float32, least / len(cuts), largest / len(cuts)))
        factor_of = factor_of * jnp.repeat(draws, shape[position] // blocks).reshape([-1 if axis == position else 1 for axis in range(len(shape))])
    return factor_of


def centred(own_key, shape, spread, most, cuts=(), kind=jnp.bfloat16):
    result = jax.random.normal(own_key, shape, jnp.float32) * spread
    if len(cuts) > 0:
        result = block_scale(own_key, shape, cuts, -0.22, 0.18) * result
    return jnp.clip(result, min=-most, max=most).astype(kind)


def setup_inputs(seed: int = 0) -> dict:
    key_list = jax.random.split(jax.random.key(seed), 6)
    front = draw_front(jax.random.fold_in(key_list[5], 71), 0)
    child_blocks = centred(key_list[1], (FRONTS, BLOCKS, FRONTS, CAP, BS, BS), 1.0, 6.0, ((0, 8), (1, 4)), jnp.float32)
    child_rows = draw_child_rows(jax.random.fold_in(key_list[5], 71), 0)
    child_cols = jax.vmap(lambda own: jax.random.permutation(own, BS))(jax.random.split(key_list[3], FRONTS * BLOCKS * FRONTS * CAP)).reshape((FRONTS, BLOCKS, FRONTS, CAP, BS)).astype(jnp.int32)
    child_counts = draw_child_counts(jax.random.fold_in(key_list[5], 71), 0)
    return {"front": front, "child_blocks": child_blocks, "child_rows": child_rows, "child_cols": child_cols, "child_counts": child_counts}


def factor_panel(column, start):
    size = column.shape[1]
    square = lax.slice_in_dim(column, start, start + size, axis=0)
    lower_factor = jnp.linalg.cholesky(square)
    diag_root = jnp.diagonal(lower_factor)
    solved = lax.linalg.triangular_solve(lower_factor, column, left_side=False, lower=True, transpose_a=True)
    solved = solved / diag_root
    row_ids = lax.broadcasted_iota(jnp.int32, solved.shape, 0)
    solved = jnp.where(row_ids >= start, solved, jnp.zeros_like(solved))
    return (solved, diag_root * diag_root)

def reference(front, child_blocks, child_rows, child_cols, child_counts):

    def assemble_factor(index):
        matrix = lax.dynamic_index_in_dim(front, index, 0, False)
        blocks_here = lax.dynamic_index_in_dim(child_blocks, index, 2, False)
        row_ids = lax.dynamic_index_in_dim(child_rows, index, 2, False)
        col_local = lax.dynamic_index_in_dim(child_cols, index, 2, False)
        counts_here = lax.dynamic_index_in_dim(child_counts, index, 2, False)
        offsets = (jnp.arange(BLOCKS, dtype=jnp.int32) * BS)[None, :, None, None]
        col_ids = col_local + offsets
        live = jnp.arange(CAP, dtype=jnp.int32)[None, None, :] < counts_here[:, :, None]
        masked = jnp.where(live[..., None, None], blocks_here, jnp.zeros_like(blocks_here))
        matrix = matrix.at[row_ids[..., :, None], col_ids[..., None, :]].add(masked)
        pivot_list = []
        for panel in range(PANELS):
            start = panel * BS
            factor, pivot = factor_panel(matrix[:, start:start + BS], start)
            later = matrix[:, start + BS:] - jnp.dot(factor * pivot, factor[start + BS:WIN].T, precision=lax.Precision.HIGHEST)
            matrix = jnp.concatenate([matrix[:, :start], factor, later], axis=1)
            pivot_list.append(pivot)
        return (matrix, jnp.concatenate(pivot_list))
    factors, pivots = lax.map(assemble_factor, jnp.arange(FRONTS, dtype=jnp.int32))
    return (factors, pivots)
```

```python
import functools

import jax
import jax.numpy as jnp
from jax import lax
from jax.experimental import pallas as pl
from jax.experimental.pallas import tpu as pltpu
from jax.sharding import PartitionSpec as P

PANELS = 2
HIGHEST = lax.Precision.HIGHEST
VMEM = pl.BlockSpec(memory_space=pltpu.VMEM)
SMEM = pl.BlockSpec(memory_space=pltpu.SMEM)
RAW_ROWS = 1536
CHUNKS = 6


def dot(a, b, lhs=1, rhs=0):
    return lax.dot_general(
        a, b, (((lhs,), (rhs,)), ((), ())), precision=HIGHEST, preferred_element_type=jnp.float32
    )


def pack_kernel(counts_ref, blocks_ref, rows_ref, cols_ref, send_ref):
    slots, width = rows_ref.shape[1], rows_ref.shape[2]
    live_slots = counts_ref[0, pl.program_id(0)]
    target_ids = lax.broadcasted_iota(jnp.int32, (width, width), 0)
    for slot in range(slots):
        columns = jnp.broadcast_to(cols_ref[0, slot : slot + 1, :], (width, width))
        placement = (columns == target_ids).astype(jnp.float32)
        placed = dot(blocks_ref[0, slot], placement, 1, 1)
        live = jnp.full((width, width), slot < live_slots)
        send_ref[0, slot, 0:width, :] = jnp.where(live, placed, jnp.zeros_like(placed))
        row_ids = rows_ref[0, slot : slot + 1, :].astype(jnp.float32)
        send_ref[0, slot, width:, :] = jnp.broadcast_to(row_ids, (8, width))


def pack(blocks, rows, cols, counts):
    groups, slots, width = rows.shape
    index_spec = pl.BlockSpec((1, slots, width), lambda g: (g, 0, 0))
    return pl.pallas_call(
        pack_kernel,
        grid=(groups,),
        in_specs=[
            SMEM,
            pl.BlockSpec((1, slots, width, width), lambda g: (g, 0, 0, 0)),
            index_spec,
            index_spec,
        ],
        out_specs=pl.BlockSpec((1, slots, width + 8, width), lambda g: (g, 0, 0, 0)),
        out_shape=jax.ShapeDtypeStruct((groups, slots, width + 8, width), jnp.float32),
        name="pack",
    )(counts, blocks, rows, cols)


def assemble_kernel(rows_ref, blocks_ref, front_ref, out_ref):
    blocks, width = rows_ref.shape
    out_ref[...] = front_ref[...]
    batch = 16

    def add_block(block, carry):
        for first in range(0, width, batch):
            targets = [rows_ref[block, first + i] for i in range(batch)]
            sums = [
                out_ref[pl.ds(targets[i], 1), :] + blocks_ref[block, first + i : first + i + 1, :]
                for i in range(batch)
            ]
            for i in range(batch):
                out_ref[pl.ds(targets[i], 1), :] = sums[i]
        return carry

    lax.fori_loop(0, blocks, add_block, 0)


def assemble(rows, blocks, front):
    return pl.pallas_call(
        assemble_kernel,
        in_specs=[SMEM, VMEM, VMEM],
        out_specs=VMEM,
        out_shape=jax.ShapeDtypeStruct(front.shape, jnp.float32),
        name="assemble",
    )(rows, blocks, front)


def eliminate(m_ref, e_ref, wt_ref):
    size = m_ref.shape[0]
    row_ids = lax.broadcasted_iota(jnp.int32, (size, size), 0)
    col_ids = lax.broadcasted_iota(jnp.int32, (size, size), 1)
    e_ref[...] = (row_ids == col_ids).astype(jnp.float32)
    sub = lax.broadcasted_iota(jnp.int32, (8, size), 0)
    lane = lax.broadcasted_iota(jnp.int32, (1, size), 1)

    def step(k, diag):
        base = pl.multiple_of(k * 8, 8)
        rm, re = m_ref[pl.ds(base, 8), :], e_ref[pl.ds(base, 8), :]
        below = row_ids > base + 7
        m, e = m_ref[...], e_ref[...]
        scale = jnp.zeros((8, size), jnp.float32)
        for j in range(8):
            row_m, row_e = rm[j : j + 1, :], re[j : j + 1, :]
            pivot = rm[j : j + 1, j : j + 1]
            inverse = 1.0 / jnp.broadcast_to(pivot, (1, size))
            diag = jnp.where(lane == base + j, jnp.broadcast_to(pivot, (1, size)), diag)
            scale = jnp.where(sub == j, inverse, scale)
            l_r = jnp.where(sub > j, jnp.broadcast_to(rm[:, j : j + 1], (8, size)) * inverse, 0.0)
            rm, re = rm - l_r * row_m, re - l_r * row_e
            l_m = jnp.where(below, jnp.broadcast_to(m[:, j : j + 1], (size, size)) * inverse, 0.0)
            m, e = m - l_m * row_m, e - l_m * row_e
        m_ref[...] = pltpu.roll(m, size - 8, 1)
        e_ref[...] = e
        e_ref[pl.ds(base, 8), :] = re
        wt_ref[pl.ds(base, 8), :] = re * scale
        return diag

    return lax.fori_loop(0, size // 8, step, jnp.zeros((1, size), jnp.float32))


def factor_kernel(
    index_ref, tops_ref, own_ref, weights_ref, top_out_ref, pivots_ref, m_ref, e_ref, wt_ref, g_ref, h_ref
):
    blocks, width = tops_ref.shape[0], tops_ref.shape[2]
    mine = index_ref[0]

    def top(panel, block):
        place = lax.rem(mine - block + blocks, blocks)
        return tops_ref[place, panel * width : (panel + 1) * width, :]

    m_ref[...] = top(0, 0)
    pivots_ref[:, 0:width] = eliminate(m_ref, e_ref, wt_ref)
    wt_0, e_0 = wt_ref[...], e_ref[...]

    def panel_0(block, carry):
        rows = top(0, block)
        g_ref[0, block] = dot(wt_0, rows)
        h_ref[0, block] = dot(e_0, rows)
        return carry

    lax.fori_loop(0, blocks, panel_0, 0)
    g_01, h_01 = g_ref[0, 1], h_ref[0, 1]
    m_ref[...] = top(1, 1) - dot(g_01, h_01, 0, 0)
    pivots_ref[:, width:] = eliminate(m_ref, e_ref, wt_ref)
    wt_1, e_1 = wt_ref[...], e_ref[...]

    def panel_1(block, carry):
        rows = top(1, block) - dot(g_01, h_ref[0, block], 0, 0)
        g_ref[1, block] = dot(wt_1, rows)
        h_ref[1, block] = dot(e_1, rows)
        return carry

    g_ref[1, 0] = jnp.zeros_like(wt_1)
    lax.fori_loop(1, blocks, panel_1, 0)

    def update_weights(slot, block):
        y_1 = dot(wt_1, h_ref[1, block], 0, 0)
        weights_ref[slot, 0:width, :] = dot(wt_0, h_ref[0, block] - dot(h_01, y_1), 0, 0)
        weights_ref[slot, width:, :] = y_1

    for slot in range(1, weights_ref.shape[0]):
        update_weights(slot, slot + 1)

    @pl.when(mine == 0)
    def _():
        weights_ref[0, 0:width, :] = jnp.zeros_like(wt_0)
        weights_ref[0, width:, :] = wt_0.T

    @pl.when(mine == 1)
    def _():
        weights_ref[0, 0:width, :] = -dot(dot(wt_0, h_01, 0, 0), wt_1, 1, 1)
        weights_ref[0, width:, :] = wt_1.T

    @pl.when(mine > 1)
    def _():
        update_weights(0, mine)

    def top_rows(block, carry):
        rows = pl.ds(pl.multiple_of(block * width, width), width)

        @pl.when(mine <= 1)
        def _():
            top_out_ref[rows, :] = g_ref[mine, block].T

        @pl.when(mine > 1)
        def _():
            update = dot(g_ref[0, block], h_ref[0, mine], 0, 0)
            update += dot(g_ref[1, block], h_ref[1, mine], 0, 0)
            top_out_ref[rows, :] = own_ref[rows, :] - update

        return carry

    lax.fori_loop(0, blocks, top_rows, 0)


def factor(index, tops, own_top, slots):
    blocks, height, width = tops.shape
    window = blocks * width
    square = pltpu.VMEM((width, width), jnp.float32)
    panels = pltpu.VMEM((PANELS, blocks, width, width), jnp.float32)
    return pl.pallas_call(
        factor_kernel,
        in_specs=[SMEM, VMEM, VMEM],
        out_specs=[VMEM, VMEM, VMEM],
        out_shape=[
            jax.ShapeDtypeStruct((slots, 2 * width, width), jnp.float32),
            jax.ShapeDtypeStruct((window, width), jnp.float32),
            jax.ShapeDtypeStruct((1, 2 * width), jnp.float32),
        ],
        scratch_shapes=[square, square, square, panels, panels],
        name="factor",
    )(index, tops, own_top)


def multiply_kernel(left_ref, right_ref, weights_ref, *out_refs):
    width = left_ref.shape[1]
    for i, out_ref in enumerate(out_refs):
        out_ref[...] = dot(left_ref[...], weights_ref[i, 0:width, :]) + dot(
            right_ref[...], weights_ref[i, width:, :]
        )


def multiply(left, right, weights):
    rows, width = left.shape
    tile = 256
    spec = pl.BlockSpec((tile, width), lambda i: (i, 0))
    count = weights.shape[0]
    return pl.pallas_call(
        multiply_kernel,
        grid=(rows // tile,),
        in_specs=[spec, spec, pl.BlockSpec(weights.shape, lambda i: (0, 0, 0))],
        out_specs=[spec] * count,
        out_shape=[jax.ShapeDtypeStruct((rows, width), jnp.float32)] * count,
        name="multiply",
    )(left, right, weights)


def per_device(front, child_blocks, child_rows, child_cols, child_counts, *, blocks):
    own = front[0]
    total, width = own.shape
    window = blocks * width
    groups, slots = child_blocks.shape[2], child_blocks.shape[3]
    mine = lax.axis_index("blk")
    index = mine.astype(jnp.int32).reshape(1)

    top = own[: 2 * width]
    tops = [top]
    for shift in range(1, blocks):
        pairs = [(i, (i + shift) % blocks) for i in range(blocks)]
        tops.append(lax.ppermute(top, "blk", pairs))

    send = pack(child_blocks[0, 0], child_rows[0, 0], child_cols[0, 0], child_counts[0])
    got = lax.all_to_all(send, "group", split_axis=0, concat_axis=0, tiled=True)
    got = got.reshape(groups * slots, width + 8, width)
    rows = got[:, width, :].astype(jnp.int32)
    assembled = assemble(rows, got, own)

    def finish(out, start, own_rows, first, update):
        mixed = jnp.where(mine <= 1, first, own_rows - update)
        return lax.dynamic_update_slice(out, mixed, (start, 0))

    rest = (total - window - RAW_ROWS) // CHUNKS
    sizes = [RAW_ROWS] + [rest] * CHUNKS
    starts = [window + sum(sizes[:i]) for i in range(len(sizes))]
    chunks = [assembled[start : start + size] for start, size in zip(starts, sizes)]

    if blocks > 4:
        weights, top_out, pivots = factor(index, jnp.stack(tops), own[:window], 1)
        out = lax.dynamic_update_slice(jnp.zeros_like(own), top_out, (0, 0))
        for start, chunk in zip(starts, chunks):
            out, chunk = lax.optimization_barrier((out, chunk))
            left, right = (
                lax.psum(jnp.where(mine == owner, chunk, 0.0), "blk") for owner in range(PANELS)
            )
            (first,) = multiply(left, jnp.where(mine == 0, chunk, right), weights)
            out = finish(out, start, chunk, first, first)
        return out[None], pivots

    raw = chunks[0]
    raw_far = lax.ppermute(raw, "blk", [(0, 2)])
    raw_near = lax.ppermute(raw, "blk", [(0, 1), (1, 2)])
    lefts = [lax.ppermute(c, "blk", [(0, 1)]) for c in chunks[1:]]

    tops, _ = lax.optimization_barrier((jnp.stack(tops), raw))
    weights, top_out, pivots = factor(index, tops, own[:window], blocks - 1)
    out = lax.dynamic_update_slice(jnp.zeros_like(own), top_out, (0, 0))

    left = jnp.where(mine == 2, raw_far, raw_near)
    right = jnp.where(mine == 2, raw_near, raw)
    first, *updates = multiply(left, right, weights)
    update = jnp.where(mine == 2, first, 0.0)
    for block in range(3, blocks):
        update += lax.ppermute(updates[block - 2], "blk", [(2, block)])
    out = finish(out, window, raw, first, update)

    for start, chunk, left in zip(starts[1:], chunks[1:], lefts):
        first, *updates = multiply(left, chunk, weights)
        update = sum(
            lax.ppermute(u, "blk", [(1, block)]) for block, u in enumerate(updates, start=2)
        )
        out = finish(out, start, chunk, first, update)
    return out[None], pivots


def solution(mesh):
    in_specs = (
        P("group", None, "blk"),
        P("group", "blk", None, None, None, None),
        P("group", "blk", None, None, None),
        P("group", "blk", None, None, None),
        P("group", "blk", None),
    )
    out_specs = (P("group", None, "blk"), P("group", None))
    return jax.shard_map(
        functools.partial(per_device, blocks=mesh.shape["blk"]),
        mesh=mesh,
        in_specs=in_specs,
        out_specs=out_specs,
        check_vma=False,
    )
```

```python
import functools

import jax
import jax.numpy as jnp
from jax import lax
from jax.experimental import pallas as pl
from jax.experimental.pallas import tpu as pltpu
from jax.sharding import PartitionSpec as P


PANELS = 2
HIGHEST = lax.Precision.HIGHEST
VMEM = pl.BlockSpec(memory_space=pltpu.VMEM)
SMEM = pl.BlockSpec(memory_space=pltpu.SMEM)
ANY = pl.BlockSpec(memory_space=pl.ANY)
RAW_ROWS = 2048
FIRST_ROWS = 512
CHUNKS = 6


def dot(a, b, lhs=1, rhs=0):
    return lax.dot_general(
        a, b, (((lhs,), (rhs,)), ((), ())), precision=HIGHEST, preferred_element_type=jnp.float32
    )


def pack_kernel(counts_ref, partners_ref, blocks_ref, rows_ref, cols_ref, *refs):
    send_refs, (staged_ref, sem) = refs[:-2], refs[-2:]
    slots, width = rows_ref.shape[1], rows_ref.shape[2]
    target_ids = lax.broadcasted_iota(jnp.int32, (width, width), 0)
    copies = [
        pltpu.make_async_copy(blocks_ref.at[partners_ref[k]], staged_ref.at[k], sem.at[k])
        for k in range(len(send_refs))
    ]
    for copy in copies:
        copy.start()
    for k, send_ref in enumerate(send_refs):
        partner = partners_ref[k]
        copies[k].wait()
        live_slots = counts_ref[0, partner]
        indices = jnp.concatenate([rows_ref[partner], cols_ref[partner]], axis=0)
        for slot in range(slots):
            columns = jnp.broadcast_to(indices[slots + slot : slots + slot + 1, :], (width, width))
            placement = (columns == target_ids).astype(jnp.float32).astype(jnp.bfloat16)
            left = staged_ref[k, slot]
            placed = jnp.zeros((width, width), jnp.float32)
            for _ in range(3):
                term = left.astype(jnp.bfloat16)
                left = left - term.astype(jnp.float32)
                placed += lax.dot_general(
                    term, placement, (((1,), (1,)), ((), ())), preferred_element_type=jnp.float32
                )
            live = jnp.full((width, width), slot < live_slots)
            base = slot * (width + 8)
            send_ref[base : base + width, :] = jnp.where(live, placed, jnp.zeros_like(placed))
            row_ids = indices[slot : slot + 1, :].astype(jnp.float32)
            send_ref[base + width : base + width + 8, :] = jnp.broadcast_to(row_ids, (8, width))


def pack(blocks, rows, cols, counts, partners):
    groups, slots, width = rows.shape
    return pl.pallas_call(
        pack_kernel,
        in_specs=[SMEM, SMEM, ANY, VMEM, VMEM],
        out_specs=[VMEM] * groups,
        out_shape=[jax.ShapeDtypeStruct((slots * (width + 8), width), jnp.float32)] * groups,
        scratch_shapes=[
            pltpu.VMEM(blocks.shape, jnp.float32),
            pltpu.SemaphoreType.DMA((groups,)),
        ],
        name="pack",
    )(counts, partners, blocks, rows, cols)


def assemble_kernel(rows_ref, front_ref, *refs, window, sources, starts):
    block_refs, out_refs = refs[:sources], refs[sources:-4]
    sums_ref, staged_ref, front_sem, sem = refs[-4:]
    width = staged_ref.shape[2]
    height = width + 8
    slots = staged_ref.shape[1] // height
    rest = front_ref.shape[0] - window
    batch = 16
    loads = [pltpu.make_async_copy(front_ref.at[pl.ds(window, rest)], sums_ref, front_sem)]
    loads += [
        pltpu.make_async_copy(ref, staged_ref.at[i], sem.at[i]) for i, ref in enumerate(block_refs)
    ]
    for copy in loads:
        copy.start()
    for copy in loads:
        copy.wait()

    def add_block(block, carry):
        source, base = block // slots, lax.rem(block, slots) * height
        for first in range(0, width, batch):
            targets = [rows_ref[block, first + i] - window for i in range(batch)]
            sums = [
                sums_ref[pl.ds(targets[i], 1), :] + staged_ref[source, pl.ds(base + first + i, 1), :]
                for i in range(batch)
            ]
            for i in range(batch):
                sums_ref[pl.ds(targets[i], 1), :] = sums[i]
        return carry

    lax.fori_loop(0, sources * slots, add_block, 0)
    stores = [
        pltpu.make_async_copy(sums_ref.at[pl.ds(start - window, ref.shape[0])], ref, sem.at[i])
        for i, (start, ref) in enumerate(zip(starts, out_refs))
    ]
    for copy in stores:
        copy.start()
    for copy in stores:
        copy.wait()


def assemble(rows, blocks, front, window, starts, sizes):
    width = front.shape[1]
    return pl.pallas_call(
        functools.partial(assemble_kernel, window=window, sources=len(blocks), starts=starts),
        in_specs=[SMEM] + [ANY] * (1 + len(blocks)),
        out_specs=[ANY] * len(sizes),
        out_shape=[jax.ShapeDtypeStruct((size, width), jnp.float32) for size in sizes],
        scratch_shapes=[
            pltpu.VMEM((front.shape[0] - window, width), jnp.float32),
            pltpu.VMEM((len(blocks),) + blocks[0].shape, jnp.float32),
            pltpu.SemaphoreType.DMA,
            pltpu.SemaphoreType.DMA((max(len(blocks), len(sizes)),)),
        ],
        name="assemble",
    )(rows, front, *blocks)


def eliminate(m_ref, e_ref, wt_ref):
    size = m_ref.shape[0]
    row_ids = lax.broadcasted_iota(jnp.int32, (size, size), 0)
    col_ids = lax.broadcasted_iota(jnp.int32, (size, size), 1)
    e_ref[...] = (row_ids == col_ids).astype(jnp.float32)
    sub = lax.broadcasted_iota(jnp.int32, (8, size), 0)
    lane = lax.broadcasted_iota(jnp.int32, (1, size), 1)

    def step(k, diag):
        base = pl.multiple_of(k * 8, 8)
        rm, re = m_ref[pl.ds(base, 8), :], e_ref[pl.ds(base, 8), :]
        below = row_ids > base + 7
        m, e = m_ref[...], e_ref[...]
        scale = jnp.zeros((8, size), jnp.float32)
        for j in range(8):
            row_m, row_e = rm[j : j + 1, :], re[j : j + 1, :]
            pivot = rm[j : j + 1, j : j + 1]
            inverse = 1.0 / jnp.broadcast_to(pivot, (1, size))
            diag = jnp.where(lane == base + j, jnp.broadcast_to(pivot, (1, size)), diag)
            scale = jnp.where(sub == j, inverse, scale)
            l_r = jnp.where(sub > j, jnp.broadcast_to(rm[:, j : j + 1], (8, size)) * inverse, 0.0)
            rm, re = rm - l_r * row_m, re - l_r * row_e
            l_m = jnp.where(below, jnp.broadcast_to(m[:, j : j + 1], (size, size)) * inverse, 0.0)
            m, e = m - l_m * row_m, e - l_m * row_e
        m_ref[...] = pltpu.roll(m, size - 8, 1)
        e_ref[...] = e
        e_ref[pl.ds(base, 8), :] = re
        wt_ref[pl.ds(base, 8), :] = re * scale
        return diag

    return lax.fori_loop(0, size // 8, step, jnp.zeros((1, size), jnp.float32))


def factor_kernel(
    index_ref, tops_ref, own_ref, weights_ref, top_out_ref, pivots_ref, m_ref, e_ref, wt_ref, g_ref, h_ref
):
    blocks, width = tops_ref.shape[0], tops_ref.shape[2]
    mine = index_ref[0]

    def top(panel, block):
        place = lax.rem(mine - block + blocks, blocks)
        return tops_ref[place, panel * width : (panel + 1) * width, :]

    m_ref[...] = top(0, 0)
    pivots_ref[:, 0:width] = eliminate(m_ref, e_ref, wt_ref)
    wt_0, e_0 = wt_ref[...], e_ref[...]

    def panel_0(block, carry):
        rows = top(0, block)
        g_ref[0, block] = dot(wt_0, rows)
        h_ref[0, block] = dot(e_0, rows)
        return carry

    lax.fori_loop(0, blocks, panel_0, 0)
    g_01, h_01 = g_ref[0, 1], h_ref[0, 1]
    m_ref[...] = top(1, 1) - dot(g_01, h_01, 0, 0)
    pivots_ref[:, width:] = eliminate(m_ref, e_ref, wt_ref)
    wt_1, e_1 = wt_ref[...], e_ref[...]

    def panel_1(block, carry):
        rows = top(1, block) - dot(g_01, h_ref[0, block], 0, 0)
        g_ref[1, block] = dot(wt_1, rows)
        h_ref[1, block] = dot(e_1, rows)
        return carry

    g_ref[1, 0] = jnp.zeros_like(wt_1)
    lax.fori_loop(1, blocks, panel_1, 0)

    def update_weights(slot, block):
        y_1 = dot(wt_1, h_ref[1, block], 0, 0)
        weights_ref[slot, 0:width, :] = dot(wt_0, h_ref[0, block] - dot(h_01, y_1), 0, 0)
        weights_ref[slot, width:, :] = y_1

    for slot in range(1, weights_ref.shape[0]):
        update_weights(slot, slot + 1)

    @pl.when(mine == 0)
    def _():
        weights_ref[0, 0:width, :] = jnp.zeros_like(wt_0)
        weights_ref[0, width:, :] = wt_0.T

    @pl.when(mine == 1)
    def _():
        weights_ref[0, 0:width, :] = -dot(dot(wt_0, h_01, 0, 0), wt_1, 1, 1)
        weights_ref[0, width:, :] = wt_1.T

    @pl.when(mine > 1)
    def _():
        update_weights(0, mine)

    def top_rows(block, carry):
        rows = pl.ds(pl.multiple_of(block * width, width), width)

        @pl.when(mine <= 1)
        def _():
            top_out_ref[rows, :] = g_ref[mine, block].T

        @pl.when(mine > 1)
        def _():
            update = dot(g_ref[0, block], h_ref[0, mine], 0, 0)
            update += dot(g_ref[1, block], h_ref[1, mine], 0, 0)
            top_out_ref[rows, :] = own_ref[rows, :] - update

        return carry

    lax.fori_loop(0, blocks, top_rows, 0)


def factor(index, tops, own_top, slots):
    blocks, _, width = tops.shape
    window = blocks * width
    square = pltpu.VMEM((width, width), jnp.float32)
    panels = pltpu.VMEM((PANELS, blocks, width, width), jnp.float32)
    return pl.pallas_call(
        factor_kernel,
        in_specs=[SMEM, VMEM, VMEM],
        out_specs=[VMEM, VMEM, VMEM],
        out_shape=[
            jax.ShapeDtypeStruct((slots, 2 * width, width), jnp.float32),
            jax.ShapeDtypeStruct((window, width), jnp.float32),
            jax.ShapeDtypeStruct((1, 2 * width), jnp.float32),
        ],
        scratch_shapes=[square, square, square, panels, panels],
        name="factor",
    )(index, tops, own_top)


def multiply_kernel(left_ref, right_ref, weights_ref, *out_refs):
    width = left_ref.shape[1]
    for i, out_ref in enumerate(out_refs):
        out_ref[...] = dot(left_ref[...], weights_ref[i, 0:width, :]) + dot(
            right_ref[...], weights_ref[i, width:, :]
        )


def multiply(left, right, weights):
    rows, width = left.shape
    tile = 256
    spec = pl.BlockSpec((tile, width), lambda i: (i, 0))
    count = weights.shape[0]
    return pl.pallas_call(
        multiply_kernel,
        grid=(rows // tile,),
        in_specs=[spec, spec, pl.BlockSpec(weights.shape, lambda i: (0, 0, 0))],
        out_specs=[spec] * count,
        out_shape=[jax.ShapeDtypeStruct((rows, width), jnp.float32)] * count,
        name="multiply",
    )(left, right, weights)


def cut_rows(first, last):
    rest = last - first - RAW_ROWS - FIRST_ROWS
    size = -(-rest // ((CHUNKS - 1) * 256)) * 256
    sizes = [RAW_ROWS, FIRST_ROWS]
    while rest > 0:
        sizes.append(min(size, rest))
        rest -= sizes[-1]
    return [first + sum(sizes[:i]) for i in range(len(sizes))], sizes


def exchange(packed, groups):
    got = []
    for distance, block in packed:
        if distance == 0:
            got.append(block)
            continue
        pairs = [(i, i ^ distance) for i in range(groups)]
        got.append(lax.ppermute(block, "group", pairs))
    return got


def per_device(front, child_blocks, child_rows, child_cols, child_counts, *, blocks):
    return extend_and_factor(front[0], child_blocks[0, 0], child_rows[0, 0], child_cols[0, 0], child_counts[0], blocks)


def extend_and_factor(own, child_blocks, child_rows, child_cols, child_counts, blocks):
    total, width = own.shape
    window = blocks * width
    groups, slots = child_rows.shape[:2]
    mine = lax.axis_index("blk")
    index = mine.astype(jnp.int32).reshape(1)

    top = own[: 2 * width]
    tops = [top]
    for shift in range(1, blocks):
        pairs = [(i, (i + shift) % blocks) for i in range(blocks)]
        tops.append(lax.ppermute(top, "blk", pairs))

    distances = sorted(range(groups), key=lambda d: (-bin(d >> 1).count("1"), -d))
    partners = jnp.array(distances, jnp.int32) ^ lax.axis_index("group").astype(jnp.int32)
    packed = pack(child_blocks, child_rows, child_cols, child_counts, partners)
    got = exchange(list(zip(distances, packed)), groups)
    row_lines = [slot * (width + 8) + width for slot in range(slots)]
    rows = jnp.concatenate([g[i : i + 1] for g in got for i in row_lines]).astype(jnp.int32)
    starts, sizes = cut_rows(window, total)
    chunks = assemble(rows, got, own, window, starts, sizes)

    def finish(out, start, own_rows, first, update):
        mixed = jnp.where(mine <= 1, first, own_rows - update)
        return lax.dynamic_update_slice(out, mixed, (start, 0))

    if blocks > 4:
        weights, top_out, pivots = factor(index, jnp.stack(tops), own[:window], 1)
        out = lax.dynamic_update_slice(jnp.zeros_like(own), top_out, (0, 0))
        for start, chunk in zip(starts, chunks):
            out, chunk = lax.optimization_barrier((out, chunk))
            left, right = (
                lax.psum(jnp.where(mine == owner, chunk, 0.0), "blk") for owner in range(PANELS)
            )
            (first,) = multiply(left, jnp.where(mine == 0, chunk, right), weights)
            out = finish(out, start, chunk, first, first)
        return out[None], pivots

    raw = chunks[0]
    raw_far = lax.ppermute(raw, "blk", [(0, 2)])
    raw_middle = lax.ppermute(raw, "blk", [(1, 2)])
    lefts = []
    for chunk in chunks[1:]:
        lefts.append(lax.ppermute(chunk, "blk", [(0, 1)]))
    raw_near = lax.ppermute(raw, "blk", [(0, 1)])

    tops, raw = lax.optimization_barrier((jnp.stack(tops), raw))
    weights, top_out, pivots = factor(index, tops, own[:window], blocks - 1)
    out = lax.dynamic_update_slice(jnp.zeros_like(own), top_out, (0, 0))

    products = []
    for chunk, left in zip(chunks[1:], lefts):
        first, *updates = multiply(left, chunk, weights)
        moved = []
        for block, u in enumerate(updates, start=2):
            moved.append(lax.ppermute(u, "blk", [(1, block)]))
        products.append((first, moved))
        weights, _ = lax.optimization_barrier((weights, first))

    raw_left = jnp.where(mine == 2, raw_far, raw_near)
    raw_right = jnp.where(mine == 2, raw_middle, raw)
    raw_first, *updates = multiply(raw_left, raw_right, weights)
    update = jnp.where(mine == 2, raw_first, 0.0)
    for block in range(3, blocks):
        update += lax.ppermute(updates[block - 2], "blk", [(2, block)])
    out = finish(out, window, raw, raw_first, update)

    for start, chunk, (first, moved) in zip(starts[1:], chunks[1:], products):
        out = finish(out, start, chunk, first, sum(moved))
    return out[None], pivots


def solution(mesh):
    in_specs = (
        P("group", None, "blk"),
        P("group", "blk", None, None, None, None),
        P("group", "blk", None, None, None),
        P("group", "blk", None, None, None),
        P("group", "blk", None),
    )
    out_specs = (P("group", None, "blk"), P("group", None))
    return jax.shard_map(
        functools.partial(per_device, blocks=mesh.shape["blk"]),
        mesh=mesh,
        in_specs=in_specs,
        out_specs=out_specs,
        check_vma=False,
    )
```

```python
import functools

import jax
import jax.numpy as jnp
from jax import lax
from jax.experimental import pallas as pl
from jax.experimental.pallas import tpu as pltpu
from jax.sharding import PartitionSpec as P


PANELS = 2
HIGHEST = lax.Precision.HIGHEST
VMEM = pl.BlockSpec(memory_space=pltpu.VMEM)
SMEM = pl.BlockSpec(memory_space=pltpu.SMEM)
ANY = pl.BlockSpec(memory_space=pl.ANY)
HBM = pl.BlockSpec(memory_space=pltpu.HBM)
RAW_ROWS = 2048
FIRST_ROWS = 512
CHUNKS = 6


def grant(mib):
    return pltpu.CompilerParams(vmem_limit_bytes=mib << 20)


def in_hbm(x):
    return pltpu.with_memory_space_constraint(x, pltpu.HBM)


def dot(a, b, lhs=1, rhs=0):
    return lax.dot_general(
        a, b, (((lhs,), (rhs,)), ((), ())), precision=HIGHEST, preferred_element_type=jnp.float32
    )


def pack_kernel(index_ref, blocks_hbm, rows_hbm, cols_hbm, counts_hbm, *refs, distances):
    send_refs, (staged_ref, rows_ref, cols_ref, counts_ref, sem) = refs[:-5], refs[-5:]
    slots, width = rows_ref.shape[1], rows_ref.shape[2]
    target_ids = lax.broadcasted_iota(jnp.int32, (width, width), 0)
    partners = [index_ref[0] ^ distance for distance in distances]
    count = len(distances)
    small = [(counts_hbm, counts_ref), (cols_hbm, cols_ref), (rows_hbm, rows_ref)]
    small = [pltpu.make_async_copy(*pair, sem.at[count + i]) for i, pair in enumerate(small)]
    copies = [
        pltpu.make_async_copy(blocks_hbm.at[partner], staged_ref.at[k], sem.at[k])
        for k, partner in enumerate(partners)
    ]
    for copy in small + copies:
        copy.start()
    for copy in small:
        copy.wait()
    for k, (partner, send_ref) in enumerate(zip(partners, send_refs)):
        copies[k].wait()
        live_slots = counts_ref[0, partner]
        rows, columns = rows_ref[partner], cols_ref[partner]
        for slot in range(slots):
            placement = jnp.broadcast_to(columns[slot : slot + 1, :], (width, width)) == target_ids
            placement = placement.astype(jnp.float32).astype(jnp.bfloat16)
            left = staged_ref[k, slot]
            placed = jnp.zeros((width, width), jnp.float32)
            for _ in range(3):
                term = left.astype(jnp.bfloat16)
                left = left - term.astype(jnp.float32)
                placed += lax.dot_general(
                    term, placement, (((1,), (1,)), ((), ())), preferred_element_type=jnp.float32
                )
            live = jnp.full((width, width), slot < live_slots)
            base = slot * (width + 8)
            send_ref[base : base + width, :] = jnp.where(live, placed, jnp.zeros_like(placed))
            row_ids = rows[slot : slot + 1, :].astype(jnp.float32)
            send_ref[base + width : base + width + 8, :] = jnp.broadcast_to(row_ids, (8, width))


def pack(blocks, rows, cols, counts, index, distances):
    slots, width = rows.shape[1:]
    count = len(distances)
    return pl.pallas_call(
        functools.partial(pack_kernel, distances=distances),
        in_specs=[SMEM] + [HBM] * 4,
        out_specs=[VMEM] * count,
        out_shape=[jax.ShapeDtypeStruct((slots * (width + 8), width), jnp.float32)] * count,
        scratch_shapes=[
            pltpu.VMEM((count,) + blocks.shape[1:], jnp.float32),
            pltpu.VMEM(rows.shape, jnp.int32),
            pltpu.VMEM(cols.shape, jnp.int32),
            pltpu.SMEM(counts.shape, jnp.int32),
            pltpu.SemaphoreType.DMA((count + 3,)),
        ],
        compiler_params=grant(8),
        name="pack",
    )(index, *(in_hbm(x) for x in (blocks, rows, cols, counts)))


def assemble_kernel(rows_ref, front_ref, *refs, window, sources):
    block_refs, out_refs, (sums_ref, sem) = refs[:sources], refs[sources:-2], refs[-2:]
    width = rows_ref.shape[1]
    slots = rows_ref.shape[0] // sources
    batch = 16
    load = pltpu.make_async_copy(front_ref.at[pl.ds(window, sums_ref.shape[0])], sums_ref, sem.at[0])
    load.start()
    load.wait()

    def add_slot(block_ref, block, base):
        for first in range(0, width, batch):
            targets = [rows_ref[block, first + i] - window for i in range(batch)]
            sums = [
                sums_ref[pl.ds(targets[i], 1), :] + block_ref[pl.ds(base + first + i, 1), :]
                for i in range(batch)
            ]
            for i in range(batch):
                sums_ref[pl.ds(targets[i], 1), :] = sums[i]

    for source, block_ref in enumerate(block_refs):

        def add(slot, carry):
            add_slot(block_ref, source * slots + slot, slot * (width + 8))
            return carry

        lax.fori_loop(0, slots, add, 0)
    copies, first = [], 0
    for i, ref in enumerate(out_refs):
        rows = pl.ds(first, ref.shape[0])
        copies.append(pltpu.make_async_copy(sums_ref.at[rows], ref, sem.at[i]))
        first += ref.shape[0]
    for copy in copies:
        copy.start()
    for copy in copies:
        copy.wait()


def assemble(rows, blocks, front, window, sizes):
    width = front.shape[1]
    held = [pltpu.with_memory_space_constraint(x, pltpu.VMEM) for x in blocks]
    return pl.pallas_call(
        functools.partial(assemble_kernel, window=window, sources=len(blocks)),
        in_specs=[SMEM, HBM] + [VMEM] * len(held),
        out_specs=[HBM] * len(sizes),
        out_shape=[pltpu.HBM((size, width), jnp.float32) for size in sizes],
        scratch_shapes=[
            pltpu.VMEM((front.shape[0] - window, width), jnp.float32),
            pltpu.SemaphoreType.DMA((len(sizes),)),
        ],
        compiler_params=grant(6),
        name="assemble",
    )(rows, in_hbm(front), *held)


def eliminate(m_ref, e_ref, wt_ref):
    size = m_ref.shape[0]
    row_ids = lax.broadcasted_iota(jnp.int32, (size, size), 0)
    col_ids = lax.broadcasted_iota(jnp.int32, (size, size), 1)
    e_ref[...] = (row_ids == col_ids).astype(jnp.float32)
    sub = lax.broadcasted_iota(jnp.int32, (8, size), 0)
    lane = lax.broadcasted_iota(jnp.int32, (1, size), 1)

    def step(k, diag):
        base = pl.multiple_of(k * 8, 8)
        rm, re = m_ref[pl.ds(base, 8), :], e_ref[pl.ds(base, 8), :]
        below = row_ids > base + 7
        m, e = m_ref[...], e_ref[...]
        scale = jnp.zeros((8, size), jnp.float32)
        for j in range(8):
            row_m, row_e = rm[j : j + 1, :], re[j : j + 1, :]
            pivot = rm[j : j + 1, j : j + 1]
            inverse = 1.0 / jnp.broadcast_to(pivot, (1, size))
            diag = jnp.where(lane == base + j, jnp.broadcast_to(pivot, (1, size)), diag)
            scale = jnp.where(sub == j, inverse, scale)
            l_r = jnp.where(sub > j, jnp.broadcast_to(rm[:, j : j + 1], (8, size)) * inverse, 0.0)
            rm, re = rm - l_r * row_m, re - l_r * row_e
            l_m = jnp.where(below, jnp.broadcast_to(m[:, j : j + 1], (size, size)) * inverse, 0.0)
            m, e = m - l_m * row_m, e - l_m * row_e
        m_ref[...] = pltpu.roll(m, size - 8, 1)
        e_ref[...] = e
        e_ref[pl.ds(base, 8), :] = re
        wt_ref[pl.ds(base, 8), :] = re * scale
        return diag

    return lax.fori_loop(0, size // 8, step, jnp.zeros((1, size), jnp.float32))


def factor_kernel(
    index_ref, tops_ref, own_ref, weights_ref, out_ref, pivots_ref, m_ref, e_ref, wt_ref, g_ref, h_ref
):
    blocks, width = tops_ref.shape[0], tops_ref.shape[2]
    mine = index_ref[0]

    def top(panel, block):
        place = lax.rem(mine - block + blocks, blocks)
        return tops_ref[place, panel * width : (panel + 1) * width, :]

    m_ref[...] = top(0, 0)
    pivots_ref[:, 0:width] = eliminate(m_ref, e_ref, wt_ref)
    wt_0, e_0 = wt_ref[...], e_ref[...]

    def panel_0(block, carry):
        rows = top(0, block)
        g_ref[0, block] = dot(wt_0, rows)
        h_ref[0, block] = dot(e_0, rows)
        return carry

    lax.fori_loop(0, blocks, panel_0, 0)
    g_01, h_01 = g_ref[0, 1], h_ref[0, 1]
    m_ref[...] = top(1, 1) - dot(g_01, h_01, 0, 0)
    pivots_ref[:, width:] = eliminate(m_ref, e_ref, wt_ref)
    wt_1, e_1 = wt_ref[...], e_ref[...]

    def panel_1(block, carry):
        rows = top(1, block) - dot(g_01, h_ref[0, block], 0, 0)
        g_ref[1, block] = dot(wt_1, rows)
        h_ref[1, block] = dot(e_1, rows)
        return carry

    g_ref[1, 0] = jnp.zeros_like(wt_1)
    lax.fori_loop(1, blocks, panel_1, 0)

    def update_weights(slot, block):
        y_1 = dot(wt_1, h_ref[1, block], 0, 0)
        weights_ref[slot, 0:width, :] = dot(wt_0, h_ref[0, block] - dot(h_01, y_1), 0, 0)
        weights_ref[slot, width:, :] = y_1

    for slot in range(1, weights_ref.shape[0]):
        update_weights(slot, slot + 1)

    @pl.when(mine == 0)
    def _():
        weights_ref[0, 0:width, :] = jnp.zeros_like(wt_0)
        weights_ref[0, width:, :] = wt_0.T

    @pl.when(mine == 1)
    def _():
        weights_ref[0, 0:width, :] = -dot(dot(wt_0, h_01, 0, 0), wt_1, 1, 1)
        weights_ref[0, width:, :] = wt_1.T

    @pl.when(mine > 1)
    def _():
        update_weights(0, mine)

    def top_rows(block, carry):
        rows = pl.ds(pl.multiple_of(block * width, width), width)

        @pl.when(mine <= 1)
        def _():
            out_ref[rows, :] = g_ref[mine, block].T

        @pl.when(mine > 1)
        def _():
            update = dot(g_ref[0, block], h_ref[0, mine], 0, 0)
            update += dot(g_ref[1, block], h_ref[1, mine], 0, 0)
            out_ref[rows, :] = own_ref[rows, :] - update

        return carry

    lax.fori_loop(0, blocks, top_rows, 0)


def factor(index, tops, own, slots):
    blocks, _, width = tops.shape
    window = blocks * width
    window_spec = pl.BlockSpec((window, width), lambda i: (0, 0))
    tops_spec = pl.BlockSpec(tops.shape, lambda i: (0, 0, 0))
    weights_spec = pl.BlockSpec((slots, 2 * width, width), lambda i: (0, 0, 0))
    pivots_spec = pl.BlockSpec((1, 2 * width), lambda i: (0, 0))
    square = pltpu.VMEM((width, width), jnp.float32)
    panels = pltpu.VMEM((PANELS, blocks, width, width), jnp.float32)
    return pl.pallas_call(
        factor_kernel,
        grid=(1,),
        in_specs=[SMEM, tops_spec, window_spec],
        out_specs=[weights_spec, window_spec, pivots_spec],
        out_shape=[
            jax.ShapeDtypeStruct((slots, 2 * width, width), jnp.float32),
            jax.ShapeDtypeStruct(own.shape, jnp.float32),
            jax.ShapeDtypeStruct((1, 2 * width), jnp.float32),
        ],
        scratch_shapes=[square, square, square, panels, panels],
        compiler_params=grant(24),
        name="factor",
    )(index, tops, own)


def multiply_kernel(left_ref, right_ref, weights_ref, *out_refs):
    width = left_ref.shape[1]
    for i, out_ref in enumerate(out_refs):
        out_ref[...] = dot(left_ref[...], weights_ref[i, 0:width, :]) + dot(
            right_ref[...], weights_ref[i, width:, :]
        )


def multiply(left, right, weights):
    rows, width = left.shape
    tile = 256
    spec = pl.BlockSpec((tile, width), lambda i: (i, 0))
    count = weights.shape[0]
    return pl.pallas_call(
        multiply_kernel,
        grid=(rows // tile,),
        in_specs=[spec, spec, pl.BlockSpec(weights.shape, lambda i: (0, 0, 0))],
        out_specs=[spec] * count,
        out_shape=[jax.ShapeDtypeStruct((rows, width), jnp.float32)] * count,
        compiler_params=grant(12),
        name="multiply",
    )(left, right, weights)


def finish_kernel(index_ref, own_ref, first_ref, *refs):
    update_refs, out_ref = refs[:-2], refs[-1]

    @pl.when(index_ref[0] < PANELS)
    def _():
        out_ref[...] = first_ref[...]

    @pl.when(index_ref[0] >= PANELS)
    def _():
        rows = own_ref[...]
        for update_ref in update_refs:
            rows = rows - update_ref[...]
        out_ref[...] = rows


def finish(index, out, start, own_rows, first, updates):
    rows, width = own_rows.shape
    tile = 256
    spec = pl.BlockSpec((tile, width), lambda i: (i, 0))
    count = 2 + len(updates)
    return pl.pallas_call(
        finish_kernel,
        grid=(rows // tile,),
        in_specs=[SMEM] + [spec] * count + [ANY],
        out_specs=pl.BlockSpec((tile, width), lambda i: (start // tile + i, 0)),
        out_shape=pltpu.HBM(out.shape, jnp.float32),
        input_output_aliases={count + 1: 0},
        compiler_params=grant(6),
        name="finish",
    )(index, own_rows, first, *updates, in_hbm(out))


def cut_rows(first, last):
    rest = last - first - RAW_ROWS - FIRST_ROWS
    size = -(-rest // ((CHUNKS - 1) * 256)) * 256
    sizes = [RAW_ROWS, FIRST_ROWS]
    while rest > 0:
        sizes.append(min(size, rest))
        rest -= sizes[-1]
    return [first + sum(sizes[:i]) for i in range(len(sizes))], sizes


def per_device(front, child_blocks, child_rows, child_cols, child_counts, *, blocks):
    return extend_and_factor(front[0], child_blocks[0, 0], child_rows[0, 0], child_cols[0, 0], child_counts[0], blocks)


def extend_and_factor(own, child_blocks, child_rows, child_cols, child_counts, blocks):
    total, width = own.shape
    window = blocks * width
    groups, slots = child_rows.shape[:2]
    mine = lax.axis_index("blk")
    index = mine.astype(jnp.int32).reshape(1)

    top = own[: 2 * width]
    tops = [top]
    for shift in range(1, blocks):
        pairs = [(i, (i + shift) % blocks) for i in range(blocks)]
        tops.append(lax.ppermute(top, "blk", pairs))

    group = lax.axis_index("group").astype(jnp.int32).reshape(1)
    distances = sorted(range(groups), key=lambda d: (-bin(d >> 1).count("1"), -d))
    got = []
    for part in [distances[:2], distances[2:]]:
        packed = pack(child_blocks, child_rows, child_cols, child_counts, group, part)
        for distance, block in zip(part, packed):
            if distance > 0:
                pairs = [(i, i ^ distance) for i in range(groups)]
                block = lax.ppermute(block, "group", pairs)
            got.append(block)
    row_lines = [slot * (width + 8) + width for slot in range(slots)]
    rows = jnp.concatenate([g[i : i + 1] for g in got for i in row_lines]).astype(jnp.int32)
    starts, sizes = cut_rows(window, total)
    chunks = assemble(rows, got, own, window, sizes)

    if blocks > 4:
        weights, out, pivots = factor(index, jnp.stack(tops), own, 1)
        for start, chunk in zip(starts, chunks):
            out, chunk = lax.optimization_barrier((out, chunk))
            left, right = (
                lax.psum(jnp.where(mine == owner, chunk, 0.0), "blk") for owner in range(PANELS)
            )
            (first,) = multiply(left, jnp.where(mine == 0, chunk, right), weights)
            out = finish(index, out, start, chunk, first, [first])
        return out[None], pivots

    raw = chunks[0]
    raw_far = lax.ppermute(raw, "blk", [(0, 2)])
    raw_middle = lax.ppermute(raw, "blk", [(1, 2)])
    lefts = []
    for chunk in chunks[1:]:
        lefts.append(lax.ppermute(chunk, "blk", [(0, 1)]))
    raw_near = lax.ppermute(raw, "blk", [(0, 1)])

    tops, raw = lax.optimization_barrier((jnp.stack(tops), raw))
    weights, out, pivots = factor(index, tops, own, blocks - 1)

    products = []
    for chunk, left in zip(chunks[1:], lefts):
        first, *updates = multiply(left, chunk, weights)
        moved = []
        for block, u in enumerate(updates, start=2):
            moved.append(lax.ppermute(u, "blk", [(1, block)]))
        products.append((first, moved))
        weights, _ = lax.optimization_barrier((weights, first))

    raw_left = jnp.where(mine == 2, raw_far, raw_near)
    raw_right = jnp.where(mine == 2, raw_middle, raw)
    raw_first, *updates = multiply(raw_left, raw_right, weights)
    moved = [jnp.where(mine == 2, raw_first, 0.0)]
    for block in range(3, blocks):
        moved.append(lax.ppermute(updates[block - 2], "blk", [(2, block)]))
    out = finish(index, out, window, raw, raw_first, moved)

    for start, chunk, (first, moved) in zip(starts[1:], chunks[1:], products):
        out = finish(index, out, start, chunk, first, moved)
    return out[None], pivots


def solution(mesh):
    in_specs = (
        P("group", None, "blk"),
        P("group", "blk", None, None, None, None),
        P("group", "blk", None, None, None),
        P("group", "blk", None, None, None),
        P("group", "blk", None),
    )
    out_specs = (P("group", None, "blk"), P("group", None))
    return jax.shard_map(
        functools.partial(per_device, blocks=mesh.shape["blk"]),
        mesh=mesh,
        in_specs=in_specs,
        out_specs=out_specs,
        check_vma=False,
    )
```

```python
import functools

import jax
import jax.numpy as jnp
from jax import lax
from jax.experimental import pallas as pl
from jax.experimental.pallas import tpu as pltpu
from jax.sharding import PartitionSpec as P


PANELS = 2
HIGHEST = lax.Precision.HIGHEST
VMEM = pl.BlockSpec(memory_space=pltpu.VMEM)
SMEM = pl.BlockSpec(memory_space=pltpu.SMEM)
ANY = pl.BlockSpec(memory_space=pl.ANY)
HBM = pl.BlockSpec(memory_space=pltpu.HBM)
RAW_ROWS = 2048
FIRST_ROWS = 512
LAST_ROWS = 256
CHUNKS = 7


def grant(mib):
    return pltpu.CompilerParams(vmem_limit_bytes=mib << 20)


def in_hbm(x):
    return pltpu.with_memory_space_constraint(x, pltpu.HBM)


def dot(a, b, lhs=1, rhs=0):
    return lax.dot_general(
        a, b, (((lhs,), (rhs,)), ((), ())), precision=HIGHEST, preferred_element_type=jnp.float32
    )


def pack_kernel(index_ref, blocks_hbm, rows_hbm, cols_hbm, counts_hbm, *refs, distances):
    send_refs, (staged_ref, rows_ref, cols_ref, counts_ref, sem) = refs[:-5], refs[-5:]
    slots, width = rows_ref.shape[1], rows_ref.shape[2]
    target_ids = lax.broadcasted_iota(jnp.int32, (width, width), 0)
    partners = [index_ref[0] ^ distance for distance in distances]
    count = len(distances)
    small = [(counts_hbm, counts_ref), (cols_hbm, cols_ref), (rows_hbm, rows_ref)]
    small = [pltpu.make_async_copy(*pair, sem.at[count + i]) for i, pair in enumerate(small)]
    copies = [
        pltpu.make_async_copy(blocks_hbm.at[partner], staged_ref.at[k], sem.at[k])
        for k, partner in enumerate(partners)
    ]
    for copy in small + copies:
        copy.start()
    for copy in small:
        copy.wait()
    for k, (partner, send_ref) in enumerate(zip(partners, send_refs)):
        copies[k].wait()
        live_slots = counts_ref[0, partner]
        rows, columns = rows_ref[partner], cols_ref[partner]
        for slot in range(slots):
            placement = jnp.broadcast_to(columns[slot : slot + 1, :], (width, width)) == target_ids
            placement = placement.astype(jnp.float32).astype(jnp.bfloat16)
            left = staged_ref[k, slot]
            placed = jnp.zeros((width, width), jnp.float32)
            for _ in range(3):
                term = left.astype(jnp.bfloat16)
                left = left - term.astype(jnp.float32)
                placed += lax.dot_general(
                    term, placement, (((1,), (1,)), ((), ())), preferred_element_type=jnp.float32
                )
            live = jnp.full((width, width), slot < live_slots)
            base = slot * (width + 8)
            send_ref[base : base + width, :] = jnp.where(live, placed, jnp.zeros_like(placed))
            row_ids = rows[slot : slot + 1, :].astype(jnp.float32)
            send_ref[base + width : base + width + 8, :] = jnp.broadcast_to(row_ids, (8, width))


def pack(blocks, rows, cols, counts, index, distances):
    slots, width = rows.shape[1:]
    count = len(distances)
    return pl.pallas_call(
        functools.partial(pack_kernel, distances=distances),
        in_specs=[SMEM] + [HBM] * 4,
        out_specs=[VMEM] * count,
        out_shape=[jax.ShapeDtypeStruct((slots * (width + 8), width), jnp.float32)] * count,
        scratch_shapes=[
            pltpu.VMEM((count,) + blocks.shape[1:], jnp.float32),
            pltpu.VMEM(rows.shape, jnp.int32),
            pltpu.VMEM(cols.shape, jnp.int32),
            pltpu.SMEM(counts.shape, jnp.int32),
            pltpu.SemaphoreType.DMA((count + 3,)),
        ],
        compiler_params=grant(8),
        name="pack",
    )(index, *(in_hbm(x) for x in (blocks, rows, cols, counts)))


def assemble_kernel(rows_ref, front_ref, *refs, window, sources):
    block_refs, out_refs = refs[:sources], refs[sources:-4]
    rows_held, delta_ref, load_sem, sem = refs[-4:]
    width = rows_ref.shape[1]
    slots = rows_ref.shape[0] // sources
    batch, tile = 16, 256
    total = delta_ref.shape[0]
    load = pltpu.make_async_copy(front_ref.at[pl.ds(window, total)], rows_held, load_sem)
    load.start()

    def clear(i, carry):
        delta_ref[pl.ds(pl.multiple_of(i * tile, tile), tile), :] = jnp.zeros((tile, width), jnp.float32)
        return carry

    lax.fori_loop(0, total // tile, clear, 0)

    def add_slot(block_ref, block, base):
        for first in range(0, width, batch):
            targets = [rows_ref[block, first + i] - window for i in range(batch)]
            sums = [
                delta_ref[pl.ds(targets[i], 1), :] + block_ref[pl.ds(base + first + i, 1), :]
                for i in range(batch)
            ]
            for i in range(batch):
                delta_ref[pl.ds(targets[i], 1), :] = sums[i]

    for source, block_ref in enumerate(block_refs):

        def add(slot, carry):
            add_slot(block_ref, source * slots + slot, slot * (width + 8))
            return carry

        lax.fori_loop(0, slots, add, 0)
    load.wait()

    def join(i, carry):
        rows = pl.ds(pl.multiple_of(i * tile, tile), tile)
        delta_ref[rows, :] = rows_held[rows, :] + delta_ref[rows, :]
        return carry

    copies, first = [], 0
    for i, ref in enumerate(out_refs):
        last = first + ref.shape[0]
        lax.fori_loop(first // tile, last // tile, join, 0)
        copies.append(pltpu.make_async_copy(delta_ref.at[pl.ds(first, ref.shape[0])], ref, sem.at[i]))
        copies[-1].start()
        first = last
    for copy in copies:
        copy.wait()


def assemble(rows, blocks, front, window, sizes):
    width = front.shape[1]
    held = [pltpu.with_memory_space_constraint(x, pltpu.VMEM) for x in blocks]
    return pl.pallas_call(
        functools.partial(assemble_kernel, window=window, sources=len(blocks)),
        in_specs=[SMEM, HBM] + [VMEM] * len(held),
        out_specs=[HBM] * len(sizes),
        out_shape=[pltpu.HBM((size, width), jnp.float32) for size in sizes],
        scratch_shapes=[
            pltpu.VMEM((front.shape[0] - window, width), jnp.float32),
            pltpu.VMEM((front.shape[0] - window, width), jnp.float32),
            pltpu.SemaphoreType.DMA,
            pltpu.SemaphoreType.DMA((len(sizes),)),
        ],
        compiler_params=grant(10),
        name="assemble",
    )(rows, in_hbm(front), *held)


def eliminate(m_ref, e_ref, wt_ref):
    size = m_ref.shape[0]
    row_ids = lax.broadcasted_iota(jnp.int32, (size, size), 0)
    col_ids = lax.broadcasted_iota(jnp.int32, (size, size), 1)
    e_ref[...] = (row_ids == col_ids).astype(jnp.float32)
    sub = lax.broadcasted_iota(jnp.int32, (8, size), 0)
    lane = lax.broadcasted_iota(jnp.int32, (1, size), 1)

    def step(k, diag):
        base = pl.multiple_of(k * 8, 8)
        rm, re = m_ref[pl.ds(base, 8), :], e_ref[pl.ds(base, 8), :]
        below = row_ids > base + 7
        m, e = m_ref[...], e_ref[...]
        scale = jnp.zeros((8, size), jnp.float32)
        for j in range(8):
            row_m, row_e = rm[j : j + 1, :], re[j : j + 1, :]
            pivot = rm[j : j + 1, j : j + 1]
            inverse = 1.0 / jnp.broadcast_to(pivot, (1, size))
            diag = jnp.where(lane == base + j, jnp.broadcast_to(pivot, (1, size)), diag)
            scale = jnp.where(sub == j, inverse, scale)
            l_r = jnp.where(sub > j, jnp.broadcast_to(rm[:, j : j + 1], (8, size)) * inverse, 0.0)
            rm, re = rm - l_r * row_m, re - l_r * row_e
            l_m = jnp.where(below, jnp.broadcast_to(m[:, j : j + 1], (size, size)) * inverse, 0.0)
            m, e = m - l_m * row_m, e - l_m * row_e
        m_ref[...] = pltpu.roll(m, size - 8, 1)
        e_ref[...] = e
        e_ref[pl.ds(base, 8), :] = re
        wt_ref[pl.ds(base, 8), :] = re * scale
        return diag

    return lax.fori_loop(0, size // 8, step, jnp.zeros((1, size), jnp.float32))


def factor_kernel(
    index_ref, tops_ref, own_ref, weights_ref, out_ref, pivots_ref, m_ref, e_ref, wt_ref, g_ref, h_ref
):
    blocks, width = tops_ref.shape[0], tops_ref.shape[2]
    mine = index_ref[0]

    def top(panel, block):
        place = lax.rem(mine - block + blocks, blocks)
        return tops_ref[place, panel * width : (panel + 1) * width, :]

    m_ref[...] = top(0, 0)
    pivots_ref[:, 0:width] = eliminate(m_ref, e_ref, wt_ref)
    wt_0, e_0 = wt_ref[...], e_ref[...]

    def panel_0(block, carry):
        rows = top(0, block)
        g_ref[0, block] = dot(wt_0, rows)
        h_ref[0, block] = dot(e_0, rows)
        return carry

    lax.fori_loop(0, blocks, panel_0, 0)
    g_01, h_01 = g_ref[0, 1], h_ref[0, 1]
    m_ref[...] = top(1, 1) - dot(g_01, h_01, 0, 0)
    pivots_ref[:, width:] = eliminate(m_ref, e_ref, wt_ref)
    wt_1, e_1 = wt_ref[...], e_ref[...]

    def panel_1(block, carry):
        rows = top(1, block) - dot(g_01, h_ref[0, block], 0, 0)
        g_ref[1, block] = dot(wt_1, rows)
        h_ref[1, block] = dot(e_1, rows)
        return carry

    g_ref[1, 0] = jnp.zeros_like(wt_1)
    lax.fori_loop(1, blocks, panel_1, 0)

    def update_weights(slot, block):
        y_1 = dot(wt_1, h_ref[1, block], 0, 0)
        weights_ref[slot, 0:width, :] = dot(wt_0, h_ref[0, block] - dot(h_01, y_1), 0, 0)
        weights_ref[slot, width:, :] = y_1

    for slot in range(1, weights_ref.shape[0]):
        update_weights(slot, slot + 1)

    @pl.when(mine == 0)
    def _():
        weights_ref[0, 0:width, :] = jnp.zeros_like(wt_0)
        weights_ref[0, width:, :] = wt_0.T

    @pl.when(mine == 1)
    def _():
        weights_ref[0, 0:width, :] = -dot(dot(wt_0, h_01, 0, 0), wt_1, 1, 1)
        weights_ref[0, width:, :] = wt_1.T

    @pl.when(mine > 1)
    def _():
        update_weights(0, mine)

    def top_rows(block, carry):
        rows = pl.ds(pl.multiple_of(block * width, width), width)

        @pl.when(mine <= 1)
        def _():
            out_ref[rows, :] = g_ref[mine, block].T

        @pl.when(mine > 1)
        def _():
            update = dot(g_ref[0, block], h_ref[0, mine], 0, 0)
            update += dot(g_ref[1, block], h_ref[1, mine], 0, 0)
            out_ref[rows, :] = own_ref[rows, :] - update

        return carry

    lax.fori_loop(0, blocks, top_rows, 0)


def factor(index, tops, own, slots):
    blocks, _, width = tops.shape
    window = blocks * width
    window_spec = pl.BlockSpec((window, width), lambda i: (0, 0))
    tops_spec = pl.BlockSpec(tops.shape, lambda i: (0, 0, 0))
    weights_spec = pl.BlockSpec((slots, 2 * width, width), lambda i: (0, 0, 0))
    pivots_spec = pl.BlockSpec((1, 2 * width), lambda i: (0, 0))
    square = pltpu.VMEM((width, width), jnp.float32)
    panels = pltpu.VMEM((PANELS, blocks, width, width), jnp.float32)
    return pl.pallas_call(
        factor_kernel,
        grid=(1,),
        in_specs=[SMEM, tops_spec, window_spec],
        out_specs=[weights_spec, window_spec, pivots_spec],
        out_shape=[
            jax.ShapeDtypeStruct((slots, 2 * width, width), jnp.float32),
            jax.ShapeDtypeStruct(own.shape, jnp.float32),
            jax.ShapeDtypeStruct((1, 2 * width), jnp.float32),
        ],
        scratch_shapes=[square, square, square, panels, panels],
        compiler_params=grant(24),
        name="factor",
    )(index, tops, own)


def multiply_kernel(left_ref, right_ref, weights_ref, *out_refs):
    width = left_ref.shape[1]
    for i, out_ref in enumerate(out_refs):
        out_ref[...] = dot(left_ref[...], weights_ref[i, 0:width, :]) + dot(
            right_ref[...], weights_ref[i, width:, :]
        )


def multiply(left, right, weights):
    rows, width = left.shape
    tile = 256
    spec = pl.BlockSpec((tile, width), lambda i: (i, 0))
    count = weights.shape[0]
    return pl.pallas_call(
        multiply_kernel,
        grid=(rows // tile,),
        in_specs=[spec, spec, pl.BlockSpec(weights.shape, lambda i: (0, 0, 0))],
        out_specs=[spec] * count,
        out_shape=[jax.ShapeDtypeStruct((rows, width), jnp.float32)] * count,
        compiler_params=grant(12),
        name="multiply",
    )(left, right, weights)


def finish_kernel(index_ref, own_ref, first_ref, *refs):
    update_refs, out_ref = refs[:-2], refs[-1]

    @pl.when(index_ref[0] < PANELS)
    def _():
        out_ref[...] = first_ref[...]

    @pl.when(index_ref[0] >= PANELS)
    def _():
        rows = own_ref[...]
        for update_ref in update_refs:
            rows = rows - update_ref[...]
        out_ref[...] = rows


def finish(index, out, start, own_rows, first, updates):
    rows, width = own_rows.shape
    tile = 256
    spec = pl.BlockSpec((tile, width), lambda i: (i, 0))
    count = 2 + len(updates)
    return pl.pallas_call(
        finish_kernel,
        grid=(rows // tile,),
        in_specs=[SMEM] + [spec] * count + [ANY],
        out_specs=pl.BlockSpec((tile, width), lambda i: (start // tile + i, 0)),
        out_shape=pltpu.HBM(out.shape, jnp.float32),
        input_output_aliases={count + 1: 0},
        compiler_params=grant(6),
        name="finish",
    )(index, own_rows, first, *updates, in_hbm(out))


def cut_rows(first, last):
    rest = last - first - RAW_ROWS - FIRST_ROWS - LAST_ROWS
    size = -(-rest // ((CHUNKS - 2) * 256)) * 256
    sizes = [RAW_ROWS, FIRST_ROWS]
    while rest > 0:
        sizes.append(min(size, rest))
        rest -= sizes[-1]
    sizes.append(LAST_ROWS)
    return [first + sum(sizes[:i]) for i in range(len(sizes))], sizes


def per_device(front, child_blocks, child_rows, child_cols, child_counts, *, blocks):
    return extend_and_factor(front[0], child_blocks[0, 0], child_rows[0, 0], child_cols[0, 0], child_counts[0], blocks)


def extend_and_factor(own, child_blocks, child_rows, child_cols, child_counts, blocks):
    total, width = own.shape
    window = blocks * width
    groups, slots = child_rows.shape[:2]
    mine = lax.axis_index("blk")
    index = mine.astype(jnp.int32).reshape(1)

    top = own[: 2 * width]
    tops = [top]
    for shift in range(1, blocks):
        pairs = [(i, (i + shift) % blocks) for i in range(blocks)]
        tops.append(lax.ppermute(top, "blk", pairs))

    group = lax.axis_index("group").astype(jnp.int32).reshape(1)
    distances = sorted(range(groups), key=lambda d: (-bin(d >> 1).count("1"), -d))
    got = []
    for part in [distances[:2], distances[2:]]:
        packed = pack(child_blocks, child_rows, child_cols, child_counts, group, part)
        for distance, block in zip(part, packed):
            if distance > 0:
                pairs = [(i, i ^ distance) for i in range(groups)]
                block = lax.ppermute(block, "group", pairs)
            got.append(block)
    row_lines = [slot * (width + 8) + width for slot in range(slots)]
    rows = jnp.concatenate([g[i : i + 1] for g in got for i in row_lines]).astype(jnp.int32)
    starts, sizes = cut_rows(window, total)
    chunks = assemble(rows, got, own, window, sizes)

    if blocks > 4:
        weights, out, pivots = factor(index, jnp.stack(tops), own, 1)
        for start, chunk in zip(starts, chunks):
            out, chunk = lax.optimization_barrier((out, chunk))
            left, right = (
                lax.psum(jnp.where(mine == owner, chunk, 0.0), "blk") for owner in range(PANELS)
            )
            (first,) = multiply(left, jnp.where(mine == 0, chunk, right), weights)
            out = finish(index, out, start, chunk, first, [first])
        return out[None], pivots

    raw = chunks[0]
    raw_far = lax.ppermute(raw, "blk", [(0, 2)])
    raw_middle = lax.ppermute(raw, "blk", [(1, 2)])
    lefts = []
    for chunk in chunks[1:]:
        lefts.append(lax.ppermute(chunk, "blk", [(0, 1)]))
    raw_near = lax.ppermute(raw, "blk", [(0, 1)])

    tops, raw = lax.optimization_barrier((jnp.stack(tops), raw))
    weights, out, pivots = factor(index, tops, own, blocks - 1)

    products = []
    for chunk, left in zip(chunks[1:], lefts):
        first, *updates = multiply(left, chunk, weights)
        moved = []
        for block, u in enumerate(updates, start=2):
            moved.append(lax.ppermute(u, "blk", [(1, block)]))
        products.append((first, moved))
        weights, _ = lax.optimization_barrier((weights, first))

    raw_left = jnp.where(mine == 2, raw_far, raw_near)
    raw_right = jnp.where(mine == 2, raw_middle, raw)
    raw_first, *updates = multiply(raw_left, raw_right, weights)
    moved = [jnp.where(mine == 2, raw_first, 0.0)]
    for block in range(3, blocks):
        moved.append(lax.ppermute(updates[block - 2], "blk", [(2, block)]))
    out = finish(index, out, window, raw, raw_first, moved)

    for start, chunk, (first, moved) in zip(starts[1:], chunks[1:], products):
        out = finish(index, out, start, chunk, first, moved)
    return out[None], pivots


def solution(mesh):
    in_specs = (
        P("group", None, "blk"),
        P("group", "blk", None, None, None, None),
        P("group", "blk", None, None, None),
        P("group", "blk", None, None, None),
        P("group", "blk", None),
    )
    out_specs = (P("group", None, "blk"), P("group", None))
    return jax.shard_map(
        functools.partial(per_device, blocks=mesh.shape["blk"]),
        mesh=mesh,
        in_specs=in_specs,
        out_specs=out_specs,
        check_vma=False,
    )
```

```python
import functools

import jax
import jax.numpy as jnp
from jax import lax
from jax.experimental import pallas as pl
from jax.experimental.pallas import tpu as pltpu
from jax.sharding import PartitionSpec as P


PANELS = 2
HIGHEST = lax.Precision.HIGHEST
VMEM = pl.BlockSpec(memory_space=pltpu.VMEM)
SMEM = pl.BlockSpec(memory_space=pltpu.SMEM)
ANY = pl.BlockSpec(memory_space=pl.ANY)
HBM = pl.BlockSpec(memory_space=pltpu.HBM)
RAW_ROWS = 2304
FIRST_ROWS = 512
LAST_ROWS = 256
CHUNKS = 7


def grant(mib):
    return pltpu.CompilerParams(vmem_limit_bytes=mib << 20)


def in_hbm(x):
    return pltpu.with_memory_space_constraint(x, pltpu.HBM)


def dot(a, b, lhs=1, rhs=0):
    return lax.dot_general(
        a, b, (((lhs,), (rhs,)), ((), ())), precision=HIGHEST, preferred_element_type=jnp.float32
    )


def pack_kernel(index_ref, blocks_hbm, rows_hbm, cols_hbm, counts_hbm, front_hbm, *refs, distances):
    send_refs, top_refs, refs = refs[: len(distances)], refs[len(distances) : -5], refs[-5:]
    (staged_ref, rows_ref, cols_ref, counts_ref, sem) = refs
    slots, width = rows_ref.shape[1], rows_ref.shape[2]
    target_ids = lax.broadcasted_iota(jnp.int32, (width, width), 0)
    partners = [index_ref[0] ^ distance for distance in distances]
    count = len(distances)
    small = [(counts_hbm, counts_ref), (cols_hbm, cols_ref), (rows_hbm, rows_ref)]
    small = [pltpu.make_async_copy(*pair, sem.at[count + i]) for i, pair in enumerate(small)]
    copies = [
        pltpu.make_async_copy(blocks_hbm.at[partner], staged_ref.at[k], sem.at[k])
        for k, partner in enumerate(partners)
    ]
    tops = [
        pltpu.make_async_copy(front_hbm.at[pl.ds(0, ref.shape[0])], ref, sem.at[count + 3]) for ref in top_refs
    ]
    for copy in small + copies + tops:
        copy.start()
    for copy in small:
        copy.wait()
    for k, (partner, send_ref) in enumerate(zip(partners, send_refs)):
        copies[k].wait()
        live_slots = counts_ref[0, partner]
        rows, columns = rows_ref[partner], cols_ref[partner]
        for slot in range(slots):
            placement = jnp.broadcast_to(columns[slot : slot + 1, :], (width, width)) == target_ids
            placement = placement.astype(jnp.float32).astype(jnp.bfloat16)
            left = staged_ref[k, slot]
            placed = jnp.zeros((width, width), jnp.float32)
            for _ in range(3):
                term = left.astype(jnp.bfloat16)
                left = left - term.astype(jnp.float32)
                placed += lax.dot_general(
                    term, placement, (((1,), (1,)), ((), ())), preferred_element_type=jnp.float32
                )
            live = jnp.full((width, width), slot < live_slots)
            base = slot * width
            send_ref[base : base + width, :] = jnp.where(live, placed, jnp.zeros_like(placed))
        row_ids = [rows, jnp.zeros((8 - slots, width), jnp.int32)]
        send_ref[slots * width :, :] = jnp.concatenate(row_ids).astype(jnp.float32)
    for copy in tops:
        copy.wait()


def pack(blocks, rows, cols, counts, front, index, distances, tops):
    slots, width = rows.shape[1:]
    count = len(distances)
    return pl.pallas_call(
        functools.partial(pack_kernel, distances=distances),
        in_specs=[SMEM] + [HBM] * 5,
        out_specs=[VMEM] * (count + tops),
        out_shape=[jax.ShapeDtypeStruct((slots * width + 8, width), jnp.float32)] * count
        + [jax.ShapeDtypeStruct((PANELS * width, width), jnp.float32)] * tops,
        scratch_shapes=[
            pltpu.VMEM((count,) + blocks.shape[1:], jnp.float32),
            pltpu.VMEM(rows.shape, jnp.int32),
            pltpu.VMEM(cols.shape, jnp.int32),
            pltpu.SMEM(counts.shape, jnp.int32),
            pltpu.SemaphoreType.DMA((count + 4,)),
        ],
        compiler_params=grant(8),
        name="pack",
    )(index, *(in_hbm(x) for x in (blocks, rows, cols, counts, front)))


def assemble_kernel(rows_ref, front_ref, *refs, start, sources):
    block_refs, out_refs = refs[:sources], refs[sources:-4]
    rows_held, delta_ref, load_sem, sem = refs[-4:]
    width = rows_ref.shape[1]
    slots = rows_ref.shape[0] // sources
    batch, tile = 16, 256
    total = rows_held.shape[0]
    load = pltpu.make_async_copy(front_ref.at[pl.ds(start, total)], rows_held, load_sem)
    load.start()

    def clear(i, carry):
        rows = pl.ds(pl.multiple_of(8 + i * tile, 8), tile)
        delta_ref[rows, :] = jnp.zeros((tile, width), jnp.float32)
        return carry

    lax.fori_loop(0, total // tile, clear, 0)
    delta_ref[0:8, :] = jnp.zeros((8, width), jnp.float32)
    delta_ref[total + 8 :, :] = jnp.zeros((8, width), jnp.float32)

    def add_slot(block_ref, block, base):
        for first in range(0, width, batch):
            targets = [rows_ref[block, first + i] for i in range(batch)]
            added = [block_ref[pl.ds(base + first + i, 1), :] for i in range(batch)]
            sums = [delta_ref[pl.ds(targets[i], 1), :] + added[i] for i in range(batch)]
            for i in range(batch):
                delta_ref[pl.ds(targets[i], 1), :] = sums[i]

    for source, block_ref in enumerate(block_refs):

        def add(slot, carry):
            add_slot(block_ref, source * slots + slot, slot * width)
            return carry

        lax.fori_loop(0, slots, add, 0)
    load.wait()

    def join(i, carry):
        offset = pl.multiple_of(i * tile, tile)
        rows_held[pl.ds(offset, tile), :] += delta_ref[pl.ds(pl.multiple_of(offset + 8, 8), tile), :]
        return carry

    copies, first = [], 0
    for i, ref in enumerate(out_refs):
        last = first + ref.shape[0]
        lax.fori_loop(first // tile, last // tile, join, 0)
        copies.append(pltpu.make_async_copy(rows_held.at[pl.ds(first, ref.shape[0])], ref, sem.at[i]))
        copies[-1].start()
        first = last
    for copy in copies:
        copy.wait()


def assemble(rows, blocks, front, start, sizes):
    width = front.shape[1]
    places = jnp.clip(rows - start, -1, sum(sizes)) + 8
    held = [pltpu.with_memory_space_constraint(x, pltpu.VMEM) for x in blocks]
    return pl.pallas_call(
        functools.partial(assemble_kernel, start=start, sources=len(blocks)),
        in_specs=[SMEM, HBM] + [VMEM] * len(held),
        out_specs=[HBM] * len(sizes),
        out_shape=[pltpu.HBM((size, width), jnp.float32) for size in sizes],
        scratch_shapes=[
            pltpu.VMEM((sum(sizes), width), jnp.float32),
            pltpu.VMEM((sum(sizes) + 16, width), jnp.float32),
            pltpu.SemaphoreType.DMA,
            pltpu.SemaphoreType.DMA((len(sizes),)),
        ],
        compiler_params=grant(10),
        name="assemble",
    )(places, in_hbm(front), *held)


def eliminate(m_ref, e_ref, wt_ref):
    size = m_ref.shape[0]
    row_ids = lax.broadcasted_iota(jnp.int32, (size, size), 0)
    col_ids = lax.broadcasted_iota(jnp.int32, (size, size), 1)
    e_ref[...] = (row_ids == col_ids).astype(jnp.float32)
    sub = lax.broadcasted_iota(jnp.int32, (8, size), 0)
    lane = lax.broadcasted_iota(jnp.int32, (1, size), 1)

    def step(k, diag):
        base = pl.multiple_of(k * 8, 8)
        rm, re = m_ref[pl.ds(base, 8), :], e_ref[pl.ds(base, 8), :]
        below = row_ids > base + 7
        m, e = m_ref[...], e_ref[...]
        scale = jnp.zeros((8, size), jnp.float32)
        for j in range(8):
            row_m, row_e = rm[j : j + 1, :], re[j : j + 1, :]
            pivot = rm[j : j + 1, j : j + 1]
            inverse = 1.0 / jnp.broadcast_to(pivot, (1, size))
            diag = jnp.where(lane == base + j, jnp.broadcast_to(pivot, (1, size)), diag)
            scale = jnp.where(sub == j, inverse, scale)
            l_r = jnp.where(sub > j, jnp.broadcast_to(rm[:, j : j + 1], (8, size)) * inverse, 0.0)
            rm, re = rm - l_r * row_m, re - l_r * row_e
            l_m = jnp.where(below, jnp.broadcast_to(m[:, j : j + 1], (size, size)) * inverse, 0.0)
            m, e = m - l_m * row_m, e - l_m * row_e
        m_ref[...] = pltpu.roll(m, size - 8, 1)
        e_ref[...] = e
        e_ref[pl.ds(base, 8), :] = re
        wt_ref[pl.ds(base, 8), :] = re * scale
        return diag

    return lax.fori_loop(0, size // 8, step, jnp.zeros((1, size), jnp.float32))


def factor_kernel(
    index_ref, tops_ref, own_ref, weights_ref, out_ref, pivots_ref, m_ref, e_ref, wt_ref, g_ref, h_ref
):
    blocks, width = tops_ref.shape[0], tops_ref.shape[2]
    mine = index_ref[0]

    def top(panel, block):
        place = lax.rem(mine - block + blocks, blocks)
        return tops_ref[place, panel * width : (panel + 1) * width, :]

    m_ref[...] = top(0, 0)
    pivots_ref[:, 0:width] = eliminate(m_ref, e_ref, wt_ref)
    wt_0, e_0 = wt_ref[...], e_ref[...]

    def panel_0(block, carry):
        rows = top(0, block)
        g_ref[0, block] = dot(wt_0, rows)
        h_ref[0, block] = dot(e_0, rows)
        return carry

    lax.fori_loop(0, blocks, panel_0, 0)
    g_01, h_01 = g_ref[0, 1], h_ref[0, 1]
    m_ref[...] = top(1, 1) - dot(g_01, h_01, 0, 0)
    pivots_ref[:, width:] = eliminate(m_ref, e_ref, wt_ref)
    wt_1, e_1 = wt_ref[...], e_ref[...]

    def panel_1(block, carry):
        rows = top(1, block) - dot(g_01, h_ref[0, block], 0, 0)
        g_ref[1, block] = dot(wt_1, rows)
        h_ref[1, block] = dot(e_1, rows)
        return carry

    g_ref[1, 0] = jnp.zeros_like(wt_1)
    lax.fori_loop(1, blocks, panel_1, 0)

    def update_weights(slot, block):
        y_1 = dot(wt_1, h_ref[1, block], 0, 0)
        weights_ref[slot, 0:width, :] = dot(wt_0, h_ref[0, block] - dot(h_01, y_1), 0, 0)
        weights_ref[slot, width:, :] = y_1

    for slot in range(1, weights_ref.shape[0]):
        update_weights(slot, slot + 1)

    @pl.when(mine == 0)
    def _():
        weights_ref[0, 0:width, :] = jnp.zeros_like(wt_0)
        weights_ref[0, width:, :] = wt_0.T

    @pl.when(mine == 1)
    def _():
        weights_ref[0, 0:width, :] = -dot(dot(wt_0, h_01, 0, 0), wt_1, 1, 1)
        weights_ref[0, width:, :] = wt_1.T

    @pl.when(mine > 1)
    def _():
        update_weights(0, mine)

    def top_rows(block, carry):
        rows = pl.ds(pl.multiple_of(block * width, width), width)

        @pl.when(mine <= 1)
        def _():
            out_ref[rows, :] = g_ref[mine, block].T

        @pl.when(mine > 1)
        def _():
            update = dot(g_ref[0, block], h_ref[0, mine], 0, 0)
            update += dot(g_ref[1, block], h_ref[1, mine], 0, 0)
            out_ref[rows, :] = own_ref[rows, :] - update

        return carry

    lax.fori_loop(0, blocks, top_rows, 0)


def factor(index, tops, own, slots):
    blocks, _, width = tops.shape
    window = blocks * width
    window_spec = pl.BlockSpec((window, width), lambda i: (0, 0))
    tops_spec = pl.BlockSpec(tops.shape, lambda i: (0, 0, 0))
    weights_spec = pl.BlockSpec((slots, 2 * width, width), lambda i: (0, 0, 0))
    pivots_spec = pl.BlockSpec((1, 2 * width), lambda i: (0, 0))
    square = pltpu.VMEM((width, width), jnp.float32)
    panels = pltpu.VMEM((PANELS, blocks, width, width), jnp.float32)
    return pl.pallas_call(
        factor_kernel,
        grid=(1,),
        in_specs=[SMEM, tops_spec, window_spec],
        out_specs=[weights_spec, window_spec, pivots_spec],
        out_shape=[
            jax.ShapeDtypeStruct((slots, 2 * width, width), jnp.float32),
            jax.ShapeDtypeStruct(own.shape, jnp.float32),
            jax.ShapeDtypeStruct((1, 2 * width), jnp.float32),
        ],
        scratch_shapes=[square, square, square, panels, panels],
        compiler_params=grant(24),
        name="factor",
    )(index, tops, own)


def multiply_kernel(left_ref, right_ref, weights_ref, *out_refs):
    width = left_ref.shape[1]
    for i, out_ref in enumerate(out_refs):
        out_ref[...] = dot(left_ref[...], weights_ref[i, 0:width, :]) + dot(
            right_ref[...], weights_ref[i, width:, :]
        )


def multiply(left, right, weights):
    rows, width = left.shape
    tile = 256
    spec = pl.BlockSpec((tile, width), lambda i: (i, 0))
    count = weights.shape[0]
    return pl.pallas_call(
        multiply_kernel,
        grid=(rows // tile,),
        in_specs=[spec, spec, pl.BlockSpec(weights.shape, lambda i: (0, 0, 0))],
        out_specs=[spec] * count,
        out_shape=[jax.ShapeDtypeStruct((rows, width), jnp.float32)] * count,
        compiler_params=grant(12),
        name="multiply",
    )(left, right, weights)


def finished(index_ref, own_ref, first_ref, update_refs, out_ref):
    mine = index_ref[0]

    @pl.when(mine < PANELS)
    def _():
        out_ref[...] = first_ref[...]

    for i, update_ref in enumerate(update_refs):

        @pl.when((mine == PANELS + i) if len(update_refs) > 1 else (mine >= PANELS))
        def _():
            out_ref[...] = own_ref[...] - update_ref[...]


def finish_kernel(index_ref, own_ref, first_ref, *refs):
    finished(index_ref, own_ref, first_ref, refs[:-2], refs[-1])


def finish(index, out, start, own_rows, first, updates):
    rows, width = own_rows.shape
    tile = 256
    spec = pl.BlockSpec((tile, width), lambda i: (i, 0))
    count = 2 + len(updates)
    return pl.pallas_call(
        finish_kernel,
        grid=(rows // tile,),
        in_specs=[SMEM] + [spec] * count + [ANY],
        out_specs=pl.BlockSpec((tile, width), lambda i: (start // tile + i, 0)),
        out_shape=pltpu.HBM(out.shape, jnp.float32),
        input_output_aliases={count + 1: 0},
        compiler_params=grant(6),
        name="finish",
    )(index, own_rows, first, *updates, in_hbm(out))


def finish_last_kernel(index_ref, own_ref, first_ref, *refs, start):
    update_refs, out_ref, (rows_ref, sem) = refs[:-4], refs[-3], refs[-2:]
    finished(index_ref, own_ref, first_ref, update_refs, rows_ref)
    copy = pltpu.make_async_copy(rows_ref, out_ref.at[pl.ds(start, rows_ref.shape[0])], sem)
    copy.start()
    copy.wait()


def finish_last(index, out, start, own_rows, first, updates):
    held = [pltpu.with_memory_space_constraint(x, pltpu.VMEM) for x in [own_rows, first, *updates]]
    return pl.pallas_call(
        functools.partial(finish_last_kernel, start=start),
        in_specs=[SMEM] + [VMEM] * len(held) + [HBM],
        out_specs=HBM,
        out_shape=pltpu.HBM(out.shape, jnp.float32),
        scratch_shapes=[pltpu.VMEM(own_rows.shape, jnp.float32), pltpu.SemaphoreType.DMA],
        input_output_aliases={len(held) + 1: 0},
        compiler_params=grant(2),
        name="finish_last",
    )(index, *held, in_hbm(out))


def cut_rows(first, last):
    rest = last - first - RAW_ROWS - FIRST_ROWS - LAST_ROWS
    size = -(-rest // ((CHUNKS - 2) * 256)) * 256
    sizes = [RAW_ROWS, FIRST_ROWS]
    while rest > 0:
        sizes.append(min(size, rest))
        rest -= sizes[-1]
    sizes.append(LAST_ROWS)
    return [first + sum(sizes[:i]) for i in range(len(sizes))], sizes


def send(x, source, target):
    return lax.ppermute(x, "blk", [(source, target)])


def per_device(front, child_blocks, child_rows, child_cols, child_counts, *, blocks):
    return extend_and_factor(front[0], child_blocks[0, 0], child_rows[0, 0], child_cols[0, 0], child_counts[0], blocks)


def extend_and_factor(own, child_blocks, child_rows, child_cols, child_counts, blocks):
    total, width = own.shape
    window = blocks * width
    groups, slots = child_rows.shape[:2]
    mine = lax.axis_index("blk")
    index = mine.astype(jnp.int32).reshape(1)

    group = lax.axis_index("group").astype(jnp.int32).reshape(1)
    distances = sorted(range(groups), key=lambda d: (-bin(d >> 1).count("1"), -(d & 1), -d))
    got = []
    for call, part in enumerate([distances[:2], distances[2:]]):
        packed = pack(child_blocks, child_rows, child_cols, child_counts, own, group, part, call)
        for distance, block in zip(part, packed):
            if distance > 0:
                pairs = [(i, i ^ distance) for i in range(groups)]
                block = lax.ppermute(block, "group", pairs)
            got.append(block)
    top = packed[-1]
    tops = [top]
    for shift in range(1, blocks):
        pairs = [(i, (i + shift) % blocks) for i in range(blocks)]
        tops.append(lax.ppermute(top, "blk", pairs))
    rows = jnp.concatenate([g[slots * width : slots * width + slots] for g in got]).astype(jnp.int32)
    starts, sizes = cut_rows(window, total)
    chunks = assemble(rows, got, own, starts[0], sizes[:2])
    chunks += assemble(rows, got, own, starts[2], sizes[2:])

    if blocks > 4:
        weights, out, pivots = factor(index, jnp.stack(tops), own, 1)
        for start, chunk in zip(starts, chunks):
            out, chunk = lax.optimization_barrier((out, chunk))
            left, right = (
                lax.psum(jnp.where(mine == owner, chunk, 0.0), "blk") for owner in range(PANELS)
            )
            (first,) = multiply(left, jnp.where(mine == 0, chunk, right), weights)
            out = finish(index, out, start, chunk, first, [first])
        return out[None], pivots

    raw = chunks[0]
    raw_far = send(raw, 0, 2)
    raw_middle = lax.ppermute(raw, "blk", [(1, 2), (2, 1)])
    lefts = []
    for chunk in chunks[1:]:
        lefts.append(send(chunk, 0, 1))
    raw_near = send(raw, 0, 1)

    tops, raw = lax.optimization_barrier((jnp.stack(tops), raw))
    weights, out, pivots = factor(index, tops, own, blocks - 1)

    products = []
    for chunk, left in zip(chunks[1:], lefts):
        first, *updates = multiply(left, chunk, weights)
        moved = []
        for block, u in enumerate(updates, start=2):
            moved.append(send(u, 1, block))
        products.append((first, moved))
        weights, _ = lax.optimization_barrier((weights, first))

    raw_left = jnp.where(mine == 2, raw_far, raw_near)
    raw_right = jnp.where(mine == 2, raw_middle, raw)
    raw_first, *updates = multiply(raw_left, raw_right, weights)
    moved = [raw_first] + [send(updates[block - 2], 2, block) for block in range(3, blocks)]
    stretches = list(zip(starts[1:], chunks[1:], products))
    stretches.insert(4, (window, raw, (raw_first, moved)))
    for start, chunk, (first, moved) in stretches[:-1]:
        out = finish(index, out, start, chunk, first, moved)
    start, chunk, (first, moved) = stretches[-1]
    out = finish_last(index, out, start, chunk, first, moved)
    return out[None], pivots


def solution(mesh):
    in_specs = (
        P("group", None, "blk"),
        P("group", "blk", None, None, None, None),
        P("group", "blk", None, None, None),
        P("group", "blk", None, None, None),
        P("group", "blk", None),
    )
    out_specs = (P("group", None, "blk"), P("group", None))
    return jax.shard_map(
        functools.partial(per_device, blocks=mesh.shape["blk"]),
        mesh=mesh,
        in_specs=in_specs,
        out_specs=out_specs,
        check_vma=False,
    )
```
